128 devices in a mesh: net: 8 (over z, core), strip: 16 (over y, x).
Axes of the slice: x: 4, y: 4, z: 4, core: 2. Of those that a mesh axis runs over, the one named last changes fastest.
Arguments:
- cond_charge: bfloat16 [3072, 32, 128], P(('net', 'strip')), may hold values from -6 to 6
- cond_live: int32 [128], P(('net', 'strip')), may hold values from 2 to 24, as said below
- near_src: int32 [3072, 16], P(('net', 'strip')), may hold values from -1 to 3071, as said below
- near_mat: bfloat16 [3072, 16, 128, 128], P(('net', 'strip')), may hold values from -0.125 to 0.125
- cond_basis: bfloat16 [3072, 16, 128], P(('net', 'strip')), may hold values from -0.5 to 0.5
- cond_rank: int32 [3072], P(('net', 'strip')), may hold values from 8 to 16
- far_src: int32 [3072, 16], P(('net', 'strip')), may hold values from -1 to 3583, as said below
- far_mat: bfloat16 [3072, 16, 16, 16], P(('net', 'strip')), may hold values from -0.375 to 0.375
- iface_charge: bfloat16 [512, 32, 128], P('strip', 'net'), may hold values from -6 to 6
- iface_near: bfloat16 [512, 3, 128, 128], P('strip'), may hold values from -0.3125 to 0.3125
- iface_basis: bfloat16 [512, 16, 128], P('strip'), may hold values from -0.5 to 0.5
- iface_rank: int32 [512], P('strip'), may hold values from 8 to 16
- iface_far_src: int32 [512, 16], P('strip'), may hold values from -1 to 3583, as said below
- iface_far_mat: bfloat16 [512, 16, 16, 16], P('strip'), may hold values from -0.375 to 0.375
Outputs:
- cond_pot: bfloat16 [3072, 32, 128], P(('net', 'strip'))
- iface_pot: bfloat16 [512, 32, 128], P('strip', 'net')
The draws below stay inside these ranges and needn't reach their ends.
Inputs may be any that keep to these rules, and one draw needn't show every extreme that they name: `cond_live`: in every draw, two devices of every net group have all 24 slots live; live slots are the first ones of a device. `near_src`: entry 0 of a row is the row's own block. Every other entry is -1 (padding, only after the used entries) or a live conductor slot of a device with the same net index as the row's device. `far_src`: each entry is -1 (padding, only after the used entries), a live conductor slot, or an interface block number. `iface_far_src`: each entry is -1 (padding, only after the used entries), a live conductor slot, or an interface block number.
All inputs are finite; a program needn't handle non-finite values.
Results may differ from the reference program's by a relative error of at most 0.0027.
Values may be sent and summed in bfloat16 or wider, within the bound.
No kernel may reach another device: no remote copies, remote signals or barrier semaphores. Data moves between devices by JAX's collectives and lax.ppermute only.
A program may use at most 128 MiB of HBM per device.

```python
import jax
import jax.numpy as jnp
from jax import lax

P_SIZE = 128
R = 16
RHS = 32
NEAR = 16
FAR = 16
CBD = 24
IBD = 32
CB = 3072
IB = 512


def live_counts(key):
    devices_all = CB // CBD
    strips_all = IB // IBD
    groups_all = devices_all // strips_all
    light = jax.random.randint(jax.random.fold_in(key, 101), (devices_all,), max(1, CBD // 12), CBD // 2 + 1)
    heavy = jax.random.randint(jax.random.fold_in(key, 102), (devices_all,), CBD // 2 + 1, CBD)
    group_keys = jax.vmap(lambda g: jax.random.fold_in(jax.random.fold_in(key, 103), g))(jnp.arange(groups_all))
    order = jax.vmap(lambda k: jax.random.permutation(k, strips_all))(group_keys).reshape(devices_all)
    counts = jnp.where(order < 2, CBD, jnp.where(order == 2, heavy, light))
    return counts.astype(jnp.int32)


def pad_tail(key, source_ids, width):
    used = jax.random.randint(key, (source_ids.shape[0], 1), width // 2, width + 1)
    return jnp.where(jnp.arange(width)[None, :] < used, source_ids, -1).astype(jnp.int32)


def draw_cond_live(key, part):
    return live_counts(key)


def draw_near_src(key, part):
    alive = live_counts(key)
    strips_all = IB // IBD
    targets = jnp.arange(CB)
    net_of = targets // CBD // strips_all
    device_pick = net_of[:, None] * strips_all + jax.random.randint(jax.random.fold_in(key, 111), (CB, NEAR), 0, strips_all)
    slot_pick = jax.random.randint(jax.random.fold_in(key, 112), (CB, NEAR), 0, 1 << 20) % alive[device_pick]
    source_ids = device_pick * CBD + slot_pick
    source_ids = jnp.concatenate([targets[:, None], source_ids[:, 1:]], 1)
    return pad_tail(jax.random.fold_in(key, 113), source_ids, NEAR)


def far_ids(key, count, salt):
    alive = live_counts(key)
    devices_all = CB // CBD
    device_pick = jax.random.randint(jax.random.fold_in(key, salt + 1), (count, FAR), 0, devices_all)
    slot_pick = jax.random.randint(jax.random.fold_in(key, salt + 2), (count, FAR), 0, 1 << 20) % alive[device_pick]
    iface_ids = CB + jax.random.randint(jax.random.fold_in(key, salt + 3), (count, FAR), 0, IB)
    to_iface = jax.random.randint(jax.random.fold_in(key, salt + 4), (count, FAR), 0, 4) == 0
    source_ids = jnp.where(to_iface, iface_ids, device_pick * CBD + slot_pick)
    return pad_tail(jax.random.fold_in(key, salt + 5), source_ids, FAR)


def draw_far_src(key, part):
    return far_ids(key, CB, 200)


def draw_iface_far_src(key, part):
    return far_ids(key, IB, 300)


def touch_ends(drawn, rng, low, largest):
    longest = drawn.shape.index(max(drawn.shape))
    spots = []
    for shift in (0, 1):
        where = [jax.random.randint(jax.random.fold_in(rng, axis), (), 0, length) for axis, length in enumerate(drawn.shape)]
        where[longest] = (where[longest] + shift) % drawn.shape[longest]
        spots.append(tuple(where))
    return drawn.at[spots[0]].set(low).at[spots[1]].set(largest)


def block_levels(own_key, dims, pieces, least, largest):
    loudness = 1.0
    for axis_at, parts in pieces:
        heights = jax.random.uniform(jax.random.fold_in(jax.random.fold_in(own_key, 6), axis_at), (parts,), jnp.float32, least / len(pieces), largest / len(pieces))
        loudness = loudness * jnp.repeat(jnp.exp(heights), dims[axis_at] // parts).reshape((-1,) + (1,) * (len(dims) - 1 - axis_at))
    return loudness


def scatter_about(key, extent, spread, reach, pieces=(), kind=jnp.bfloat16):
    loudness = block_levels(key, extent, pieces, -0.22, 0.18) if pieces else 1.0
    values = jax.random.normal(key, extent, jnp.float32) * spread * loudness
    return jnp.minimum(jnp.maximum(values, -reach), reach).astype(kind)


def setup_inputs(seed: int = 0) -> dict:
    seeds = jax.random.split(jax.random.key(seed), 15)
    cond_charge = scatter_about(seeds[0], (CB, RHS, P_SIZE), 1.0, 6.0, ((0, 128),))
    cond_live = draw_cond_live(jax.random.fold_in(seeds[14], 71), 0)
    near_src = draw_near_src(jax.random.fold_in(seeds[14], 71), 0)
    near_mat = scatter_about(seeds[3], (CB, NEAR, P_SIZE, P_SIZE), (NEAR * P_SIZE) ** -0.5, 0.125, ((0, 128),))
    cond_basis = scatter_about(seeds[4], (CB, R, P_SIZE), P_SIZE ** -0.5, 0.5, ((0, 128),))
    cond_rank = touch_ends(jax.random.randint(seeds[5], (CB,), R // 2, R + 1), jax.random.fold_in(seeds[5], 1), R // 2, R).astype(jnp.int32)
    far_src = draw_far_src(jax.random.fold_in(seeds[14], 71), 0)
    far_mat = scatter_about(seeds[7], (CB, FAR, R, R), (FAR * R) ** -0.5, 0.375, ((0, 128),))
    iface_charge = scatter_about(seeds[8], (IB, RHS, P_SIZE), 1.0, 6.0, ((0, 16), (1, 8)))
    iface_near = scatter_about(seeds[9], (IB, 3, P_SIZE, P_SIZE), (3 * P_SIZE) ** -0.5, 0.3125, ((0, 16),))
    iface_basis = scatter_about(seeds[10], (IB, R, P_SIZE), P_SIZE ** -0.5, 0.5, ((0, 16),))
    iface_rank = touch_ends(jax.random.randint(seeds[11], (IB,), R // 2, R + 1), jax.random.fold_in(seeds[11], 1), R // 2, R).astype(jnp.int32)
    iface_far_src = draw_iface_far_src(jax.random.fold_in(seeds[14], 71), 0)
    iface_far_mat = scatter_about(seeds[13], (IB, FAR, R, R), (FAR * R) ** -0.5, 0.375, ((0, 16),))
    return dict(cond_charge=cond_charge, cond_live=cond_live, near_src=near_src, near_mat=near_mat, cond_basis=cond_basis, cond_rank=cond_rank, far_src=far_src, far_mat=far_mat, iface_charge=iface_charge, iface_near=iface_near, iface_basis=iface_basis, iface_rank=iface_rank, iface_far_src=iface_far_src, iface_far_mat=iface_far_mat)


def coeffs(block_basis, charge, block_rank):
    product = jnp.einsum('tap,trp->tar', block_basis.astype(jnp.float32), charge.astype(jnp.float32))
    keep_rows = (jnp.arange(R)[None, :] < block_rank[:, None]).astype(jnp.float32)
    return (product * keep_rows[:, :, None]).astype(jnp.bfloat16)


def far_field(source_ids, far_mats, block_basis, block_rank, coef_table, group_size):
    groups = source_ids.shape[0] // group_size

    def per_group(inputs):
        ids_group, mats_group, basis_group, rank_group = inputs
        usable = (ids_group >= 0).astype(jnp.float32)
        fetched = coef_table[jnp.clip(ids_group, 0, None)].astype(jnp.float32) * usable[:, :, None, None]
        gathered_far = jnp.einsum('tkab,tkbr->tar', mats_group.astype(jnp.float32), fetched)
        keep_rows = (jnp.arange(R)[None, :] < rank_group[:, None]).astype(jnp.float32)
        gathered_far = (gathered_far * keep_rows[:, :, None]).astype(jnp.bfloat16)
        return jnp.einsum('tap,tar->trp', basis_group.astype(jnp.float32), gathered_far.astype(jnp.float32))

    stacked = (source_ids.reshape(groups, group_size, -1),
               far_mats.reshape((groups, group_size) + far_mats.shape[1:]),
               block_basis.reshape((groups, group_size) + block_basis.shape[1:]),
               block_rank.reshape(groups, group_size))
    result = lax.map(per_group, stacked)
    return result.reshape((groups * group_size,) + result.shape[2:])


def near_field(near_src, near_mat, cond_charge):
    groups = near_src.shape[0] // CBD

    def per_group(inputs):
        ids_group, mats_group = inputs
        usable = (ids_group >= 0).astype(jnp.float32)
        fetched = cond_charge[jnp.clip(ids_group, 0, None)].astype(jnp.float32) * usable[:, :, None, None]
        return jnp.einsum('tkpq,tkrq->trp', mats_group.astype(jnp.float32), fetched)

    stacked = (near_src.reshape(groups, CBD, -1), near_mat.reshape((groups, CBD) + near_mat.shape[1:]))
    result = lax.map(per_group, stacked)
    return result.reshape((groups * CBD,) + result.shape[2:])


def reference(cond_charge, cond_live, near_src, near_mat, cond_basis, cond_rank, far_src, far_mat,
              iface_charge, iface_near, iface_basis, iface_rank, iface_far_src, iface_far_mat):
    coef_table = jnp.concatenate([coeffs(cond_basis, cond_charge, cond_rank),
                                  coeffs(iface_basis, iface_charge, iface_rank)], 0)
    slots = jnp.arange(CB)
    alive = (slots % CBD < cond_live[slots // CBD]).astype(jnp.float32)
    near_cond = near_field(near_src, near_mat, cond_charge)
    far_cond = far_field(far_src, far_mat, cond_basis, cond_rank, coef_table, CBD)
    cond_pot = ((near_cond + far_cond) * alive[:, None, None]).astype(jnp.bfloat16)
    charges = iface_charge.astype(jnp.float32)
    zero_block = jnp.zeros_like(charges[:1])
    before = jnp.concatenate([zero_block, charges[:-1]], 0)
    after = jnp.concatenate([charges[1:], zero_block], 0)
    couplings = iface_near.astype(jnp.float32)
    near_iface = jnp.einsum('tpq,trq->trp', couplings[:, 0], before)
    near_iface = near_iface + jnp.einsum('tpq,trq->trp', couplings[:, 1], charges)
    near_iface = near_iface + jnp.einsum('tpq,trq->trp', couplings[:, 2], after)
    far_iface = far_field(iface_far_src, iface_far_mat, iface_basis, iface_rank, coef_table, IBD)
    iface_pot = (near_iface + far_iface).astype(jnp.bfloat16)
    return cond_pot, iface_pot
```

```python
import functools

import jax
import jax.numpy as jnp
from jax import lax
from jax.experimental import pallas as pl
from jax.experimental.pallas import tpu as pltpu
from jax.sharding import Mesh, PartitionSpec as P

ALL = ("z", "core", "y", "x")
BF, F32, I32 = jnp.bfloat16, jnp.float32, jnp.int32
CBD, IBD, R, RHS, NEAR, FAR = 24, 32, 16, 32, 16, 16
HALF = CBD // 2
ROWS = 120
SMEM = pl.BlockSpec(memory_space=pltpu.SMEM)
VMEM = pl.BlockSpec(memory_space=pltpu.VMEM)
ANY = pl.BlockSpec(memory_space=pl.ANY)


def exchange(dim0, mask0, dim1, mask1):
    pairs = []
    for d in range(128):
        z, c, y, x = d >> 5, (d >> 4) & 1, (d >> 2) & 3, d & 3
        dim, mask = (dim0, mask0) if c == 0 else (dim1, mask1)
        z ^= mask if dim == "z" else 0
        y ^= mask if dim == "y" else 0
        x ^= mask if dim == "x" else 0
        pairs.append((d, ((z * 2 + c) * 4 + y) * 4 + x))
    return pairs


A_STEPS = [("x", 1, "x", 3), ("x", 3, "x", 1), ("y", 1, "y", 3), ("y", 3, "y", 1)]
B_STEPS = [("y", 1, "y", 3), ("y", 3, "y", 1), ("x", 1, "x", 3), ("x", 3, "x", 1)]
PARTNER = [(d, d ^ 16) for d in range(128)]


def coef_kernel(crank, irank, cc, cb, ic, ib, out, pay, x4, sems):
    lane = lax.broadcasted_iota(I32, (R, 128), 1)
    row = lax.broadcasted_iota(I32, (R, 128), 0)
    nt = (((1,), (1,)), ((), ()))
    for g in range(CBD // 4):
        q = cc[4 * g : 4 * g + 4].reshape(4 * RHS, 128)
        b = cb[4 * g : 4 * g + 4].reshape(4 * R, 128)
        full = lax.dot_general(b, q, nt, preferred_element_type=F32)
        tile = jnp.zeros((R, 128), F32)
        for j in range(4):
            keep = (lane // RHS == j) & (row < crank[4 * g + j])
            tile = jnp.where(keep, full[R * j : R * j + R], tile)
        pay[R * g : R * g + R, :] = tile.astype(BF)
    for i in range(IBD):
        x4[4 * i : 4 * i + 4, :] = ic[i].astype(F32)
    x = x4[...].astype(BF)
    full = lax.dot_general(ib[...].reshape(IBD * R, 128), x, nt, preferred_element_type=F32)
    tile = jnp.zeros((R, 128), F32)
    for i in range(IBD):
        keep = (lane // 4 == i) & (row < irank[i])
        tile = jnp.where(keep, full[R * i : R * i + R], tile)
    pay[96:112, :] = tile.astype(BF)
    pay[112:120, :] = jnp.concatenate([x4[0:4, :], x4[124:128, :]], 0).astype(BF)
    copies = [pltpu.make_async_copy(pay, out.at[d], sems.at[d]) for d in range(64)]
    for copy in copies:
        copy.start()
    for copy in copies:
        copy.wait()


def coef_call(crank, irank, cc, cb, ic, ib):
    return pl.pallas_call(
        coef_kernel,
        out_shape=jax.ShapeDtypeStruct((64, ROWS, 128), BF),
        in_specs=[SMEM, SMEM, VMEM, VMEM, VMEM, VMEM],
        out_specs=ANY,
        scratch_shapes=[
            pltpu.VMEM((ROWS, 128), BF),
            pltpu.VMEM((128, 128), F32),
            pltpu.SemaphoreType.DMA((64,)),
        ],
        cost_estimate=pl.CostEstimate(flops=40_000_000, bytes_accessed=3_000_000, transcendentals=0),
        name="coefs",
    )(crank, irank, cc, cb, ic, ib)


def iface_near_kernel(ic, nm, out, x4):
    nt = (((1,), (1,)), ((), ()))
    blocks = nm.shape[0]
    step = pl.program_id(0)
    x4[0:8, :] = jnp.zeros((8, 128), F32)
    x4[136:144, :] = jnp.zeros((8, 128), F32)
    for i in range(IBD):
        x4[8 + 4 * i : 12 + 4 * i, :] = ic[i].astype(F32)
    for j in range(blocks):
        base = 8 + 4 * (step * blocks + j)
        acc = jnp.zeros((4, 128), F32)
        for m in range(3):
            x = x4[pl.ds(base + 4 * (m - 1), 4), :].astype(BF)
            acc = acc + lax.dot_general(x, nm[j, m], nt, preferred_element_type=F32)
        out[4 * j : 4 * j + 4, :] = acc


def iface_near_call(ic, nm):
    blocks = 8
    return pl.pallas_call(
        iface_near_kernel,
        grid=(IBD // blocks,),
        out_shape=jax.ShapeDtypeStruct((128, 128), F32),
        in_specs=[
            pl.BlockSpec((IBD, 4, 128), lambda i: (0, 0, 0)),
            pl.BlockSpec((blocks, 3, 128, 128), lambda i: (i, 0, 0, 0)),
        ],
        out_specs=pl.BlockSpec((4 * blocks, 128), lambda i: (i, 0)),
        scratch_shapes=[pltpu.VMEM((144, 128), F32)],
        cost_estimate=pl.CostEstimate(flops=50_000_000, bytes_accessed=6_000_000, transcendentals=0),
        name="iface_near",
    )(ic, nm)


def near_kernel(idx, a0, a1, b0, b1, nm, out, tab, sems):
    step = pl.program_id(0)
    blocks = nm.shape[0]

    @pl.when(step == 0)
    def _():
        copies = [
            pltpu.make_async_copy(src, tab.at[pl.ds(96 * i, 96)], sems.at[i])
            for i, src in enumerate((a0, a1, b0, b1))
        ]
        for copy in copies:
            copy.start()
        tab[384] = jnp.zeros((RHS, 128), BF)
        for copy in copies:
            copy.wait()

    for j in range(blocks):
        t = step * blocks + j
        x = jnp.concatenate([tab[idx[k, t]] for k in range(NEAR)], 1)
        w = jnp.concatenate([nm[j, k] for k in range(NEAR)], 1)
        out[j] = lax.dot_general(x, w, (((1,), (1,)), ((), ())), preferred_element_type=F32)


def near_call(idx, pieces, nm):
    blocks = 4
    return pl.pallas_call(
        near_kernel,
        grid=(CBD // blocks,),
        out_shape=jax.ShapeDtypeStruct((CBD, RHS, 128), F32),
        in_specs=[SMEM, ANY, ANY, ANY, ANY]
        + [pl.BlockSpec((blocks, NEAR, 128, 128), lambda i: (i, 0, 0, 0))],
        out_specs=pl.BlockSpec((blocks, RHS, 128), lambda i: (i, 0, 0)),
        scratch_shapes=[pltpu.VMEM((385, RHS, 128), BF), pltpu.SemaphoreType.DMA((4,))],
        cost_estimate=pl.CostEstimate(flops=400_000_000, bytes_accessed=20_000_000, transcendentals=0),
        name="near",
    )(idx, *pieces, nm)


def far_kernel(
    tile_c, lg_c, tile_i, lg_i, crank, irank, where_am_i, live,
    own, other, near, inear, fm, ifm, cb, ib, edge0, edge1, perm,
    cpot, ipot, tab, utab, gi, xi, sems,
):
    net, strip, core = where_am_i[0], where_am_i[1], where_am_i[2]
    mine = where_am_i[3]
    copies = [
        pltpu.make_async_copy(src, tab.at[i], sems.at[i]) for i, src in enumerate((own, other))
    ]
    for copy in copies:
        copy.start()
    lane = lax.broadcasted_iota(I32, (R, 128), 1)
    row = lax.broadcasted_iota(I32, (R, 128), 0)
    group = lane // RHS
    nt = (((1,), (1,)), ((), ()))
    tn = (((0,), (0,)), ((), ()))
    for copy in copies:
        copy.wait()
    for s in range(16):
        xi[R * s : R * s + R, :] = jnp.concatenate(
            [tab[jnp.bitwise_xor(n & 1, core), (n >> 1) * 16 + s, 96:112, :] for n in range(8)], 1
        )
    u = jnp.dot(xi[...], perm[...], preferred_element_type=F32).astype(BF)
    for s in range(16):
        for j in range(8):
            utab[s * 8 + j] = u[R * s : R * s + R, 128 * j : 128 * j + 128]

    def sums(tiles, groups, mats, t):
        parts = []
        for k in range(FAR):
            where, lg = tiles[k, t], groups[k, t]
            raw = utab[where]
            parts.append(jnp.where(group == lg, raw, jnp.zeros_like(raw)))
        stacked = jnp.concatenate(parts, 0)
        return jnp.dot(mats, stacked, preferred_element_type=F32)

    def fold(v):
        v = v + pltpu.roll(v, 64, 1)
        return v + pltpu.roll(v, 32, 1)

    zero = jnp.zeros((R, 128), F32)
    for d in range(128):
        for g in range(6):
            utab[128 + d * 6 + g] = tab[d // 64, d % 64, R * g : R * g + R, :]
    for q in range(CBD // 4):
        rows = []
        for j in range(4):
            t = 4 * q + j
            v = fold(sums(tile_c, lg_c, fm[t], t))
            rows.append(jnp.where((group == j) & (row < crank[t]), v, zero))
        gmat = jnp.concatenate(rows, 0).astype(BF)
        basis = cb[4 * q : 4 * q + 4].reshape(4 * R, 128)
        far = lax.dot_general(gmat, basis, tn, preferred_element_type=F32)
        for j in range(4):
            t = 4 * q + j
            alive = jnp.where(t < live[0], 1.0, 0.0)
            cpot[t] = ((near[t] + far[RHS * j : RHS * j + RHS]) * alive).astype(BF)
    for t in range(IBD):
        v = fold(sums(tile_i, lg_i, ifm[t], t))
        v = pltpu.roll(v, lax.rem(4 * t - 4 * net + 128, 128), 1)
        gi[R * t : R * t + R, :] = jnp.where((lane // 4 == t) & (row < irank[t]), v, zero).astype(BF)
    far = lax.dot_general(gi[...], ib[...].reshape(IBD * R, 128), tn, preferred_element_type=F32)
    total = far + inear[...]
    before = tab[0, jnp.maximum(mine - 1, 0), 112:120, :].astype(F32)
    after = tab[0, jnp.minimum(mine + 1, 63), 112:120, :].astype(F32)
    before = jnp.where(strip > 0, before, 0.0).astype(BF)
    after = jnp.where(strip < 15, after, 0.0).astype(BF)
    head = lax.dot_general(before, edge0[...], nt, preferred_element_type=F32)
    tail = lax.dot_general(after, edge1[...], nt, preferred_element_type=F32)
    for t in range(IBD):
        v = total[4 * t : 4 * t + 4]
        if t == 0:
            v = v + head[4:8]
        if t == IBD - 1:
            v = v + tail[0:4]
        ipot[t] = v.astype(BF)


def far_call(scalars, arrays):
    return pl.pallas_call(
        far_kernel,
        out_shape=(
            jax.ShapeDtypeStruct((CBD, RHS, 128), BF),
            jax.ShapeDtypeStruct((IBD, 4, 128), BF),
        ),
        in_specs=[SMEM] * 8 + [ANY, ANY] + [VMEM] * 9,
        out_specs=(VMEM, VMEM),
        scratch_shapes=[
            pltpu.VMEM((2, 64, ROWS, 128), BF),
            pltpu.VMEM((896, R, 128), BF),
            pltpu.VMEM((IBD * R, 128), BF),
            pltpu.VMEM((256, 1024), BF),
            pltpu.SemaphoreType.DMA((2,)),
        ],
        cost_estimate=pl.CostEstimate(flops=1_000_000_000, bytes_accessed=12_000_000, transcendentals=0),
        name="far",
    )(*scalars, *arrays)


def far_index(ids, core):
    dev, slot = ids // CBD, ids % CBD
    half = jnp.bitwise_xor((dev >> 4) & 1, core)
    dev64 = (dev >> 5) * 16 + (dev & 15)
    cond = 128 + (half * 64 + dev64) * 6 + (slot >> 2)
    i = ids - 128 * CBD
    iface = (i >> 5) * 8 + ((i & 31) >> 2)
    is_iface = ids >= 128 * CBD
    tile = jnp.where(is_iface, iface, cond)
    group = jnp.where(is_iface, i & 3, slot & 3)
    return jnp.where(ids < 0, 0, tile), jnp.where(ids < 0, -1, group)


def near_index(ids, core, y, x, net):
    local = ids - net * (16 * CBD)
    dev, slot = local // CBD, local % CBD

    def place(off):
        g = jnp.bitwise_xor(off, off >> 1)
        return jnp.where(core == 0, g, ((g & 1) << 1) | (g >> 1))

    py = place(jnp.bitwise_xor(dev >> 2, y))
    px = place(jnp.bitwise_xor(dev & 3, x))
    at_a = (py * 4 + px) * HALF + slot
    at_b = 192 + (px * 4 + py) * HALF + slot - HALF
    return jnp.where(ids < 0, 384, jnp.where(slot < HALF, at_a, at_b))


def shards(
    cond_charge, cond_live, near_src, near_mat, cond_basis, cond_rank, far_src, far_mat,
    iface_charge, iface_near, iface_basis, iface_rank, iface_far_src, iface_far_mat,
):
    z, core, y, x = (lax.axis_index(a) for a in ALL)
    net, strip = z * 2 + core, y * 4 + x
    swap = lambda v, step: lax.ppermute(v, ALL, exchange(*step))
    a, b = cond_charge[:HALF], cond_charge[HALF:]
    pieces = []
    for n, (sa, sb) in enumerate(zip(A_STEPS, B_STEPS)):
        ra, rb = swap(a, sa), swap(b, sb)
        if n == 3:
            pieces = [a, ra, b, rb]
        else:
            a, b = jnp.concatenate([a, ra], 0), jnp.concatenate([b, rb], 0)
    pay = coef_call(cond_rank, iface_rank, cond_charge, cond_basis, iface_charge, iface_basis)
    own = lax.all_to_all(pay, ("z", "y", "x"), 0, 0, tiled=True)
    other = lax.ppermute(own, ALL, PARTNER)
    inear = iface_near_call(iface_charge, iface_near)
    nidx = near_index(near_src.T, core, y, x, net)
    tile_c, lg_c = far_index(far_src.T, core)
    tile_i, lg_i = far_index(iface_far_src.T, core)
    fm = far_mat.transpose(0, 2, 1, 3).reshape(CBD, R, FAR * R)
    ifm = iface_far_mat.transpose(0, 2, 1, 3).reshape(IBD, R, FAR * R)
    r = lax.broadcasted_iota(I32, (1024, 1024), 0)
    c = lax.broadcasted_iota(I32, (1024, 1024), 1)
    target = ((r >> 4) & 7) * 128 + ((r >> 2) & 3) * 32 + (r >> 7) * 4 + (r & 3)
    perm = (c == target).astype(BF)
    near = near_call(nidx, pieces, near_mat)
    me = jnp.stack([net, strip, core, z * 16 + strip]).astype(I32)
    return far_call(
        (tile_c, lg_c, tile_i, lg_i, cond_rank, iface_rank, me, cond_live),
        (own, other, near, inear, fm, ifm, cond_basis, iface_basis,
         iface_near[0, 0], iface_near[IBD - 1, 2], perm),
    )


def solution(mesh):
    grid = Mesh(mesh.devices.reshape(4, 2, 4, 4), ALL)
    net, strip = ("z", "core"), ("y", "x")
    every = lambda n: P(ALL, *(None,) * (n - 1))
    by_strip = lambda n: P(strip, *(None,) * (n - 1))
    return jax.shard_map(
        shards,
        mesh=grid,
        in_specs=(
            every(3), every(1), every(2), every(4), every(3), every(1), every(2), every(4),
            P(strip, net, None), by_strip(4), by_strip(3), by_strip(1), by_strip(2), by_strip(4),
        ),
        out_specs=(every(3), P(strip, net, None)),
        check_vma=False,
    )
```
